32 devices in a mesh: grp: 8 (over z, core), head: 4 (over y, x).
Axes of the slice: x: 2, y: 2, z: 4, core: 2. Of those that a mesh axis runs over, the one named last changes fastest.
Arguments:
- hidden: bfloat16 [64, 5376], P('grp'), may hold values from -6 to 6
- pre_gain: float32 [5376], replicated, may hold values from 0.5 to 1.5
- query_weight: bfloat16 [5376, 4096], P(None, 'head'), may hold values from -0.078125 to 0.078125
- key_weight: bfloat16 [5376, 2048], P(None, 'head'), may hold values from -0.078125 to 0.078125
- value_weight: bfloat16 [5376, 2048], P(None, 'head'), may hold values from -0.078125 to 0.078125
- out_weight: bfloat16 [4096, 5376], P('head'), may hold values from -0.09375 to 0.09375
- query_norm_gain: float32 [128], replicated, may hold values from 0.1 to 1.9
- key_gain: float32 [128], replicated, may hold values from 0.1 to 1.9
- post_gain: float32 [5376], P('head'), may hold values from 0.1 to 1.9
- text_keys: bfloat16 [64, 1024, 2048], P('grp', None, 'head'), may hold values from -360 to 360
- text_values: bfloat16 [64, 1024, 2048], P('grp', None, 'head'), may hold values from -6 to 6
- text_position: int32 [64], P('grp'), may hold values from 1 to 4095
- image_keys: bfloat16 [192, 256, 2048], P('grp', None, 'head'), may hold values from -360 to 360
- image_values: bfloat16 [192, 256, 2048], P('grp', None, 'head'), may hold values from -6 to 6
- image_owner: int32 [64], replicated, may hold values from 0 to 7, as said below
- image_slot: int32 [64], replicated, may hold values from 0 to 23, as said below
- image_count: int32 [64], replicated, may hold values from 128 to 256, as said below
Outputs:
- updated: bfloat16 [64, 5376], P('grp', 'head')
The draws below stay inside these ranges and needn't reach their ends.
Inputs may be any that keep to these rules, and one draw needn't show every extreme that they name: `image_owner`: each group owns at most 24 requests, and some group owns exactly 24. `image_slot`: requests with the same owner have distinct slots. `image_count`: A multiple of 128.
All inputs are finite; a program needn't handle non-finite values.
Results may differ from the reference program's by a relative error of at most 0.0055.
The reference program's roundings to bfloat16 on the way count: a program that leaves them out, or rounds other values in their place, can miss the bound.
Values may be sent and summed in bfloat16 or wider, within the bound.
No kernel may reach another device: no remote copies, remote signals or barrier semaphores. Data moves between devices by JAX's collectives and lax.ppermute only.
A program may use at most 192 MiB of HBM per device.

```python
import math
import jax
import jax.numpy as jnp
from jax import lax

D = 5376
QH = 32
KVH = 16
HD = 128
WINDOW = 1024
IMG = 256
IMG_BLOCK = 128
SLOTS = 24
BATCH = 64
SLOTS_ALL = 192
N_GRP = 8


def scaled_keys(key, count, length, width):
    base = jnp.clip(jax.random.normal(key, (count, length, width), jnp.float32), -6.0, 6.0)
    return base.astype(jnp.bfloat16)


def draw_text_keys(key, part):
    return scaled_keys(jax.random.fold_in(key, 3), BATCH, WINDOW, KVH * HD)


def draw_image_keys(key, part):
    return scaled_keys(jax.random.fold_in(key, 5), SLOTS_ALL, IMG, KVH * HD)


def owner_table(key):
    base = jax.random.fold_in(key, 11)
    hottest = jax.random.randint(base, (), 0, N_GRP)
    order = jax.random.permutation(jax.random.fold_in(base, 1), BATCH)
    ranking = jnp.zeros((BATCH,), jnp.int32).at[order].set(jnp.arange(BATCH, dtype=jnp.int32))
    remain = jnp.maximum(ranking - SLOTS, 0)
    others = (hottest + 1 + remain % (N_GRP - 1)) % N_GRP
    owners = jnp.where(ranking < SLOTS, hottest, others).astype(jnp.int32)
    owner_matches = (owners[:, None] == jnp.arange(N_GRP, dtype=jnp.int32)[None, :]).astype(jnp.int32)
    earlier = jnp.cumsum(owner_matches, 0) - owner_matches
    slotted = jnp.sum(earlier * owner_matches, 1).astype(jnp.int32)
    return (owners, slotted)


def draw_image_owner(key, part):
    return owner_table(key)[0]


def draw_image_slot(key, part):
    return owner_table(key)[1]


def draw_image_count(key, part):
    blocks = jax.random.randint(jax.random.fold_in(key, 13), (BATCH,), 1, IMG // IMG_BLOCK + 1)
    return (blocks * IMG_BLOCK).astype(jnp.int32)


def set_ends(values, rng, low, largest):
    extent = values.shape
    spot = [jax.random.randint(jax.random.fold_in(rng, axis), (), 0, extent[axis]) for axis in range(len(extent))]
    values = values.at[tuple(spot)].set(low)
    longest = extent.index(max(extent))
    spot[longest] = (spot[longest] + 1) % extent[longest]
    return values.at[tuple(spot)].set(largest)


def block_levels(stream_key, shape, pieces, least, top_value):
    def one(dim, shards_of):
        steps = jax.random.uniform(jax.random.fold_in(jax.random.fold_in(stream_key, 6), dim), (shards_of,), jnp.float32, least / len(pieces), top_value / len(pieces))
        return jnp.repeat(jnp.exp(steps), shape[dim] // shards_of).reshape((-1,) + (1,) * (len(shape) - dim - 1))

    level = one(*pieces[0])
    for cut in pieces[1:]:
        level = level * one(*cut)
    return level


def noise(rng, dims, spread, reach, cuts=(), held_as=jnp.bfloat16):
    values = spread * jax.random.normal(rng, dims, jnp.float32)
    if cuts:
        values = values * block_levels(rng, dims, cuts, -0.22, 0.18)
    return jnp.clip(values, -reach, reach).astype(held_as)


def setup_inputs(seed: int = 0) -> dict:
    splits = jax.random.split(jax.random.key(seed), 18)
    hidden = noise(splits[0], (BATCH, D), 1.0, 6.0, ((0, 8),))
    pre_gain = jnp.clip(1.0 + 0.1 * jax.random.normal(splits[1], (D,), jnp.float32), 0.5, 1.5)
    query_weight = noise(splits[2], (D, QH * HD), D ** -0.5, 0.078125, ((1, 4),))
    key_weight = noise(splits[3], (D, KVH * HD), D ** -0.5, 0.078125, ((1, 4),))
    value_weight = noise(splits[4], (D, KVH * HD), D ** -0.5, 0.078125, ((1, 4),))
    out_weight = noise(splits[5], (QH * HD, D), (QH * HD) ** -0.5, 0.09375, ((0, 4),))
    query_norm_gain = jnp.clip(1.0 + 0.18 * jax.random.normal(splits[6], (HD,), jnp.float32), 0.1, 1.9)
    key_gain = jnp.clip(1.0 + 0.18 * jax.random.normal(splits[7], (HD,), jnp.float32), 0.1, 1.9)
    post_gain = jnp.clip(1.0 + 0.18 * jax.random.normal(splits[8], (D,), jnp.float32), 0.1, 1.9)
    text_keys = draw_text_keys(jax.random.fold_in(splits[17], 71), 0)
    text_values = noise(splits[10], (BATCH, WINDOW, KVH * HD), 1.0, 6.0, ((0, 8), (2, 4)))
    text_position = set_ends(jax.random.randint(splits[11], (BATCH,), 1, 4 * WINDOW), jax.random.fold_in(splits[11], 1), 1, (4 * WINDOW) - 1).astype(jnp.int32)
    image_keys = draw_image_keys(jax.random.fold_in(splits[17], 71), 0)
    image_values = noise(splits[13], (SLOTS_ALL, IMG, KVH * HD), 1.0, 6.0, ((0, 8), (2, 4)))
    image_owner = draw_image_owner(jax.random.fold_in(splits[17], 71), 0)
    image_slot = draw_image_slot(jax.random.fold_in(splits[17], 71), 0)
    image_count = draw_image_count(jax.random.fold_in(splits[17], 71), 0)
    return dict(hidden=hidden, pre_gain=pre_gain, query_weight=query_weight, key_weight=key_weight, value_weight=value_weight, out_weight=out_weight, query_norm_gain=query_norm_gain, key_gain=key_gain, post_gain=post_gain, text_keys=text_keys, text_values=text_values, text_position=text_position, image_keys=image_keys, image_values=image_values, image_owner=image_owner, image_slot=image_slot, image_count=image_count)


EPS = 1e-06

def norm_rows(values, gain):
    values = values.astype(jnp.float32)
    mean_sq = lax.optimization_barrier(jnp.mean(values * values, axis=-1, keepdims=True))
    return values * lax.rsqrt(mean_sq + EPS) * gain.astype(jnp.float32)

def rotate(values, position):
    half = values.shape[-1] // 2
    freq = jnp.exp(-jnp.log(1000000.0) * jnp.arange(half, dtype=jnp.float32) / half)
    angle = position.astype(jnp.float32)[:, None] * freq[None, :]
    cosine = jnp.cos(angle)[:, None, :]
    sine = jnp.sin(angle)[:, None, :]
    first = values[..., :half]
    second = values[..., half:]
    return jnp.concatenate([first * cosine - second * sine, second * cosine + first * sine], axis=-1)

def weigh(scores, valid):
    scores = jnp.where(valid, scores, -1e+30)
    top = lax.optimization_barrier(jnp.max(scores, -1))
    weights = jnp.where(valid, jnp.exp(scores - top[..., None]), 0.0).astype(jnp.bfloat16)
    return (top, weights, lax.optimization_barrier(jnp.sum(weights.astype(jnp.float32), -1)))

def request_block(query_vector, keys, values, valid):
    length = keys.shape[0]
    heads, head_dim = (query_vector.shape[0], query_vector.shape[2])
    keys4 = keys.reshape(length, heads, head_dim).astype(jnp.float32)
    values4 = values.reshape(length, heads, head_dim).astype(jnp.float32)
    scores = jnp.einsum('kgd,lkd->kgl', query_vector.astype(jnp.float32), keys4)
    top, weights, total = weigh(scores, valid[None, None, :])
    summed = jnp.einsum('kgl,lkd->kgd', weights.astype(jnp.float32), values4)
    return (top, total, summed)

def combine(parts, own_token_score, self_value):
    top = own_token_score
    for part in parts:
        top = jnp.maximum(top, part[0])
    total = jnp.exp(own_token_score - top)
    summed = self_value.astype(jnp.float32)[:, :, None, :] * total[..., None]
    for part_top, part_total, part_sum in parts:
        factor = jnp.exp(part_top - top)
        total = total + part_total * factor
        summed = summed + part_sum * factor[..., None]
    return summed / total[..., None]

def reference(hidden, pre_gain, query_weight, key_weight, value_weight, out_weight, query_norm_gain, key_gain, post_gain, text_keys, text_values, text_position, image_keys, image_values, image_owner, image_slot, image_count):
    group = QH // KVH
    normed = norm_rows(hidden, pre_gain).astype(jnp.bfloat16)
    query_vector = jnp.dot(normed, query_weight, preferred_element_type=jnp.float32).reshape(BATCH, QH, HD)
    query_vector = rotate(norm_rows(query_vector, query_norm_gain), text_position) * (1.0 / math.sqrt(D // QH))
    query_vector = query_vector.astype(jnp.bfloat16).reshape(BATCH, KVH, group, HD)
    fresh_key = jnp.dot(normed, key_weight, preferred_element_type=jnp.float32).reshape(BATCH, KVH, HD)
    fresh_key = rotate(norm_rows(fresh_key, key_gain), text_position).astype(jnp.bfloat16)
    value_new = jnp.dot(normed, value_weight, preferred_element_type=jnp.float32).astype(jnp.bfloat16).reshape(BATCH, KVH, HD)
    own_token_score = jnp.einsum('fyeh,fyh->fye', query_vector.astype(jnp.float32), fresh_key.astype(jnp.float32))
    places = jnp.arange(WINDOW, dtype=jnp.int32)
    text_valid = (places[None, :] < text_position[:, None]) & (places[None, :] != (text_position % WINDOW)[:, None])
    text_part = lax.map(lambda item: request_block(*item), (query_vector, text_keys, text_values, text_valid))
    stored = (image_owner * SLOTS + image_slot).astype(jnp.int32)
    image_valid = jnp.arange(IMG, dtype=jnp.int32)[None, :] < image_count[:, None]

    def image_request(item):
        single_query, index, valid = item
        return request_block(single_query, image_keys[index], image_values[index], valid)
    image_part = lax.map(image_request, (query_vector, stored, image_valid))
    attended = combine((image_part, text_part), own_token_score, value_new).astype(jnp.bfloat16).reshape(BATCH, QH * HD)
    projected = jnp.dot(attended, out_weight, preferred_element_type=jnp.float32)
    return (hidden.astype(jnp.float32) + norm_rows(projected, post_gain)).astype(jnp.bfloat16)
```

```python
import functools
import math

import jax
import jax.numpy as jnp
from jax import lax
from jax.experimental import pallas as pl
from jax.experimental.pallas import tpu as pltpu
from jax.sharding import PartitionSpec as P

EPS = 1e-06
NEG = -1e30
BLOCK = 128
F32 = jnp.float32
BF16 = jnp.bfloat16
ANY = pl.BlockSpec(memory_space=pl.ANY)
VMEM = pl.BlockSpec(memory_space=pltpu.VMEM)
SMEM = pl.BlockSpec(memory_space=pltpu.SMEM)


def cost(flops, nbytes):
    return pl.CostEstimate(flops=flops, bytes_accessed=nbytes, transcendentals=0)


def pieces_of(rows, most):
    for size in range(most, 0, -16):
        if rows % size == 0:
            return size
    return rows


def row_copies(src, dst, sems, size):
    return [
        pltpu.make_async_copy(
            src.at[pl.ds(i * size, size)], dst.at[pl.ds(i * size, size)], sems.at[i]
        )
        for i in range(src.shape[0] // size)
    ]


def rms_rope(v, gain, cosine, sine):
    mean_sq = jnp.mean(v * v, axis=-1, keepdims=True)
    v = v * lax.rsqrt(mean_sq + EPS) * gain
    return v * cosine + pltpu.roll(v, v.shape[-1] // 2, 1) * sine


def query_kernel(
    scale, size, hidden, gain, cosine, sine, q_gain, weight, q_out, normed_out,
    w_buf, h_buf, g_buf, heads_buf, w_sem, s_sem
):
    copies = row_copies(weight, w_buf, w_sem, size)
    small = [
        pltpu.make_async_copy(hidden, h_buf, s_sem.at[0]),
        pltpu.make_async_copy(gain, g_buf, s_sem.at[1]),
    ]
    for c in small:
        c.start()
    for c in copies:
        c.start()
    for c in small:
        c.wait()
    h = h_buf[...].astype(F32)
    mean_sq = jnp.mean(h * h, axis=-1, keepdims=True)
    normed_out[...] = (h * lax.rsqrt(mean_sq + EPS) * g_buf[...]).astype(BF16)
    acc = jnp.zeros((h.shape[0], weight.shape[1]), F32)
    for i, c in enumerate(copies):
        c.wait()
        acc = acc + jnp.dot(
            normed_out[:, i * size : (i + 1) * size],
            w_buf[i * size : (i + 1) * size, :],
            preferred_element_type=F32,
        )
    dim = q_gain.shape[-1]
    for n in range(acc.shape[1] // dim):
        v = rms_rope(acc[:, n * dim : (n + 1) * dim], q_gain[...], cosine[...], sine[...])
        heads_buf[:, n, :] = v * scale
    q_out[...] = heads_buf[...].astype(BF16)


def kv_kernel(
    size, normed, cosine, sine, k_gain, q, k_weight, v_weight, self_out, v_out,
    k_buf, vw_buf, heads_buf, k_sem, v_sem
):
    k_copies = row_copies(k_weight, k_buf, k_sem, size)
    v_copies = row_copies(v_weight, vw_buf, v_sem, size)
    for a, b in zip(k_copies, v_copies):
        a.start()
        b.start()
    k_acc = jnp.zeros((normed.shape[0], k_weight.shape[1]), F32)
    v_acc = jnp.zeros((normed.shape[0], v_weight.shape[1]), F32)
    for i, (a, b) in enumerate(zip(k_copies, v_copies)):
        x = normed[:, i * size : (i + 1) * size]
        a.wait()
        k_acc = k_acc + jnp.dot(
            x, k_buf[i * size : (i + 1) * size, :], preferred_element_type=F32
        )
        b.wait()
        v_acc = v_acc + jnp.dot(
            x, vw_buf[i * size : (i + 1) * size, :], preferred_element_type=F32
        )
    dim = k_gain.shape[-1]
    heads = q.shape[1]
    group = heads // (k_acc.shape[1] // dim)
    for n in range(heads):
        if n % group == 0:
            part = slice((n // group) * dim, (n // group + 1) * dim)
            k = rms_rope(k_acc[:, part], k_gain[...], cosine[...], sine[...])
            k = k.astype(BF16).astype(F32)
            v = v_acc[:, part].astype(BF16).astype(F32)
        heads_buf[:, n, :] = k
        v_out[:, n, :] = v
    score = jnp.sum(q[...].astype(F32) * heads_buf[...], axis=-1, keepdims=True)
    self_out[...] = jnp.broadcast_to(score, self_out.shape)


def spread(q, kv_heads):
    group = q.shape[0] // kv_heads
    owner = lax.broadcasted_iota(jnp.int32, q.shape, 0) // group
    q = q.astype(F32)
    return jnp.concatenate(
        [jnp.where(owner == n, q, 0.0) for n in range(kv_heads)], axis=1
    ).astype(BF16)


def gather_heads(o, heads, dim):
    kv_heads = o.shape[1] // dim
    owner = lax.broadcasted_iota(jnp.int32, (heads, dim), 0) // (heads // kv_heads)
    total = jnp.zeros((heads, dim), F32)
    for n in range(kv_heads):
        total = jnp.where(owner == n, o[:, n * dim : (n + 1) * dim], total)
    return total


def attend(q, keys, values, valid):
    heads, dim = q.shape
    kv_heads = keys.shape[1] // dim
    scores = lax.dot_general(
        spread(q, kv_heads), keys, (((1,), (1,)), ((), ())), preferred_element_type=F32
    )
    scores = jnp.where(valid, scores, NEG)
    top = jnp.max(scores, axis=-1, keepdims=True)
    weights = jnp.where(valid, jnp.exp(scores - top), 0.0).astype(BF16)
    total = jnp.sum(weights.astype(F32), axis=-1, keepdims=True)
    summed = jnp.dot(weights, values, preferred_element_type=F32)
    return top, total, gather_heads(summed, heads, dim)


def text_kernel(
    first, count, together, position, q, keys, values, o_out, m_out, l_out, k_buf, v_buf, k_sem, v_sem
):
    window = keys.shape[1]
    k_copies = [
        pltpu.make_async_copy(keys.at[first + i], k_buf.at[i], k_sem.at[i]) for i in range(count)
    ]
    v_copies = [
        pltpu.make_async_copy(values.at[first + i], v_buf.at[i], v_sem.at[i]) for i in range(count)
    ]
    for a, b in zip(k_copies, v_copies):
        a.start()
        b.start()
    slot = lax.broadcasted_iota(jnp.int32, (q.shape[1], window), 1)
    for base in range(0, count, together):
        part = range(base, min(base + together, count))
        for i in part:
            k_copies[i].wait()
        for i in part:
            v_copies[i].wait()
        for i in part:
            p = position[first + i]
            valid = (slot < p) & (slot != lax.rem(p, window))
            top, total, summed = attend(q[first + i], k_buf[i], v_buf[i], valid)
            o_out[i] = summed
            m_out[i] = jnp.broadcast_to(top, summed.shape)
            l_out[i] = jnp.broadcast_to(total, summed.shape)


def image_kernel(
    together, owner, slot, count, *refs
):
    n_q = len(refs) - 10
    queries = refs[:n_q]
    keys, values, mine, other, k_buf, v_buf, item, filled, k_sem, v_sem = refs[n_q:]
    me = lax.axis_index("grp")
    batch = owner.shape[0]
    rows = queries[0].shape[0]
    heads, dim = queries[0].shape[1:]
    slots, length = k_buf.shape[0], k_buf.shape[1]
    levels = length // BLOCK
    mine[...] = jnp.zeros_like(mine)
    other[...] = jnp.zeros_like(other)
    for level in range(levels):
        filled[level] = 0

    def copies(place, source, block):
        span = pl.ds(block * BLOCK, BLOCK)
        return (
            pltpu.make_async_copy(
                keys.at[source, span], k_buf.at[place, span], k_sem.at[place, block]
            ),
            pltpu.make_async_copy(
                values.at[source, span], v_buf.at[place, span], v_sem.at[place, block]
            ),
        )

    def begin(r, place):
        is_mine = owner[r] == me

        @pl.when(is_mine)
        def _():
            blocks = count[r] // BLOCK
            level = blocks - 1
            n = filled[level]
            item[level, n] = r
            filled[level] = n + 1
            for block in range(levels):
                @pl.when(block < blocks)
                def _():
                    for c in copies(slot[r], slot[r], block):
                        c.start()

        return place

    lax.fori_loop(0, batch, begin, 0)

    column = lax.broadcasted_iota(jnp.int32, (heads, dim), 1)

    for level in range(levels):
        blocks = level + 1
        full = blocks * BLOCK
        have = filled[level]
        always = jnp.full((heads, full), True)

        def some(step, carry, level=level, blocks=blocks, full=full, have=have, always=always):
            todo = []
            for u in range(together):
                n = step * together + u
                r = item[level, jnp.minimum(n, have - 1)]
                todo.append((n < have, r, slot[r]))
            for live, r, place in todo:
                @pl.when(live)
                def _():
                    for block in range(blocks):
                        for c in copies(place, place, block):
                            c.wait()
            for live, r, place in todo:
                from_me = lax.bitwise_xor(r // rows, me)
                lane = lax.rem(r, rows)
                q = queries[0][lane]
                at = 1
                for ref in queries[1:]:
                    groups = ref.shape[0] // rows
                    inside = jnp.clip(from_me - at, 0, groups - 1)
                    hit = (from_me >= at) & (from_me < at + groups)
                    q = jnp.where(hit, ref[inside * rows + lane], q)
                    at += groups
                top, total, summed = attend(
                    q, k_buf[place, :full, :], v_buf[place, :full, :], always
                )
                mean = (summed / total).astype(BF16)
                level_sum = top + jnp.log(total)
                high = level_sum.astype(BF16).astype(F32)
                middle = (level_sum - high).astype(BF16).astype(F32)
                low = level_sum - high - middle
                at_lane = column - 3 * lane
                stats = jnp.where(
                    at_lane == 0,
                    high,
                    jnp.where(at_lane == 1, middle, jnp.where(at_lane == 2, low, 0.0)),
                )
                outer = from_me // 2
                same = lax.rem(from_me, 2) == 0
                for keep, ref in ((same, mine), (jnp.logical_not(same), other)):
                    @pl.when(live & keep)
                    def _():
                        ref[outer, lane] = mean
                        ref[outer, rows] = (ref[outer, rows].astype(F32) + stats).astype(BF16)
            return carry

        lax.fori_loop(0, (have + together - 1) // together, some, 0)


def out_kernel(size, n_image, *refs):
    images = refs[:n_image]
    o_text, m_text, l_text, own, v_new, weight, sent, kept, w_buf, heads_buf, at_buf, sem = refs[n_image:]
    copies = row_copies(weight, w_buf, sem, size)
    for c in copies:
        c.start()
    rows, heads, dim = o_text.shape
    stats = images[0][rows].astype(F32)
    for ref in images[1:]:
        stats = stats + ref[rows].astype(F32)
    for r in range(rows):
        mean = images[0][r].astype(F32)
        for ref in images[1:]:
            mean = mean + ref[r].astype(F32)
        image_level = (
            stats[:, 3 * r : 3 * r + 1] + stats[:, 3 * r + 1 : 3 * r + 2]
        ) + stats[:, 3 * r + 2 : 3 * r + 3]
        m = m_text[r]
        s = own[r]
        top = jnp.maximum(jnp.maximum(image_level, m), s)
        e_image = jnp.exp(image_level - top)
        e_text = jnp.exp(m - top)
        e_own = jnp.exp(s - top)
        upper = mean * e_image + o_text[r] * e_text + v_new[r] * e_own
        lower = e_image + l_text[r] * e_text + e_own
        heads_buf[r] = upper / lower
    for n in range(heads):
        at_buf[:, n * dim : (n + 1) * dim] = heads_buf[:, n, :].astype(BF16)
    for i, c in enumerate(copies):
        c.wait()
        part = jnp.dot(
            at_buf[:, i * size : (i + 1) * size],
            w_buf[i * size : (i + 1) * size, :],
            preferred_element_type=F32,
        )
        if i == 0:
            kept[...] = part
        else:
            kept[...] += part
    sent[...] = kept[...].astype(BF16)


def final_kernel(n_others, *refs):
    others = refs[:n_others]
    kept, hidden, gain, out = refs[n_others:]
    y = kept[...]
    for ref in others:
        y = y + ref[...].astype(F32)
    mean_sq = jnp.sum(y * y, axis=-1, keepdims=True) / y.shape[1]
    scale = lax.rsqrt(mean_sq + EPS)
    width = out.shape[1]
    me = lax.axis_index("head")
    for n in range(y.shape[1] // width):
        @pl.when(me == n)
        def _():
            part = slice(n * width, (n + 1) * width)
            out[...] = (hidden[:, part].astype(F32) + y[:, part] * scale * gain[...]).astype(BF16)


def swap(x, axis, k):
    n = lax.axis_size(axis)
    return lax.ppermute(x, axis, [(i, i ^ k) for i in range(n)])


def local(
    hidden, pre_gain, query_weight, key_weight, value_weight, out_weight, query_norm_gain, key_gain,
    post_gain, text_keys, text_values, text_position, image_keys, image_values, image_owner,
    image_slot, image_count,
):
    rows, width = hidden.shape
    dim = query_norm_gain.shape[0]
    heads = query_weight.shape[1] // dim
    kv_width = key_weight.shape[1]
    groups = lax.axis_size("grp")
    head_parts = lax.axis_size("head")
    scale = 1.0 / math.sqrt(width // (heads * head_parts))
    half = dim // 2
    freq = jnp.exp(-jnp.log(1000000.0) * jnp.arange(half, dtype=F32) / half)
    angle = text_position.astype(F32)[:, None] * freq[None, :]
    c, s = jnp.cos(angle), jnp.sin(angle)
    cosine = jnp.concatenate([c, c], axis=-1)
    sine = jnp.concatenate([-s, s], axis=-1)
    params = functools.partial(pltpu.CompilerParams)

    size = pieces_of(width, 768)
    n_copies = width // size
    q, normed = pl.pallas_call(
        functools.partial(query_kernel, scale, size),
        out_shape=(
            jax.ShapeDtypeStruct((rows, heads, dim), BF16),
            jax.ShapeDtypeStruct((rows, width), BF16),
        ),
        in_specs=[ANY, ANY, VMEM, VMEM, VMEM, ANY],
        out_specs=(VMEM, VMEM),
        scratch_shapes=[
            pltpu.VMEM(query_weight.shape, BF16),
            pltpu.VMEM(hidden.shape, BF16),
            pltpu.VMEM((1, width), F32),
            pltpu.VMEM((rows, heads, dim), F32),
            pltpu.SemaphoreType.DMA((n_copies,)),
            pltpu.SemaphoreType.DMA((2,)),
        ],
        compiler_params=params(vmem_limit_bytes=24 << 20),
        cost_estimate=cost(2 * rows * query_weight.size, 2 * query_weight.size),
        name="query",
    )(hidden, pre_gain.reshape(1, -1), cosine, sine, query_norm_gain.reshape(1, -1), query_weight)

    queries = [q]
    held = q
    k = 1
    while k < groups:
        got = swap(held, "grp", k)
        queries.append(got)
        k *= 2
        if k < groups:
            held = jnp.concatenate([held, got], axis=0)

    own_score, v_new = pl.pallas_call(
        functools.partial(kv_kernel, size),
        out_shape=(jax.ShapeDtypeStruct((rows, heads, dim), F32),) * 2,
        in_specs=[VMEM, VMEM, VMEM, VMEM, VMEM, ANY, ANY],
        out_specs=(VMEM, VMEM),
        scratch_shapes=[
            pltpu.VMEM(key_weight.shape, BF16),
            pltpu.VMEM(value_weight.shape, BF16),
            pltpu.VMEM((rows, heads, dim), F32),
            pltpu.SemaphoreType.DMA((n_copies,)),
            pltpu.SemaphoreType.DMA((n_copies,)),
        ],
        compiler_params=params(vmem_limit_bytes=24 << 20),
        cost_estimate=cost(4 * rows * key_weight.size, 4 * key_weight.size),
        name="keyvalue",
    )(normed, cosine, sine, key_gain.reshape(1, -1), q, key_weight, value_weight)

    window = text_keys.shape[1]
    o_text, m_text, l_text = pl.pallas_call(
        functools.partial(text_kernel, 0, rows, 2),
        out_shape=(jax.ShapeDtypeStruct((rows, heads, dim), F32),) * 3,
        in_specs=[SMEM, VMEM, ANY, ANY],
        out_specs=(VMEM,) * 3,
        scratch_shapes=[
            pltpu.VMEM((rows, window, kv_width), BF16),
            pltpu.VMEM((rows, window, kv_width), BF16),
            pltpu.SemaphoreType.DMA((rows,)),
            pltpu.SemaphoreType.DMA((rows,)),
        ],
        compiler_params=params(vmem_limit_bytes=28 << 20),
        cost_estimate=cost(8 * heads * text_keys.size, 4 * text_keys.size),
        name="text",
    )(text_position, q, text_keys, text_values)

    slots, length = image_keys.shape[0], image_keys.shape[1]
    outer = groups // 2
    mine, other = pl.pallas_call(
        functools.partial(image_kernel, 4),
        out_shape=(jax.ShapeDtypeStruct((outer, rows + 1, heads, dim), BF16),) * 2,
        in_specs=[SMEM] * 3 + [VMEM] * len(queries) + [ANY, ANY],
        out_specs=(VMEM, VMEM),
        scratch_shapes=[
            pltpu.VMEM(image_keys.shape, BF16),
            pltpu.VMEM(image_keys.shape, BF16),
            pltpu.SMEM((length // BLOCK, slots), jnp.int32),
            pltpu.SMEM((length // BLOCK,), jnp.int32),
            pltpu.SemaphoreType.DMA((slots, length // BLOCK)),
            pltpu.SemaphoreType.DMA((slots, length // BLOCK)),
        ],
        compiler_params=params(vmem_limit_bytes=24 << 20),
        cost_estimate=cost(8 * heads * image_keys.size, 4 * image_keys.size),
        name="image",
    )(image_owner, image_slot, image_count, *queries, image_keys, image_values)

    merged = mine + swap(other, "grp", 1)
    images = [merged[0]] + [swap(merged[j], "grp", 2 * j) for j in range(1, outer)]

    o_size = pieces_of(out_weight.shape[0], 256)
    sent, kept = pl.pallas_call(
        functools.partial(out_kernel, o_size, outer),
        out_shape=(
            jax.ShapeDtypeStruct((rows, width), BF16),
            jax.ShapeDtypeStruct((rows, width), F32),
        ),
        in_specs=[VMEM] * (outer + 5) + [ANY],
        out_specs=(VMEM, VMEM),
        scratch_shapes=[
            pltpu.VMEM(out_weight.shape, BF16),
            pltpu.VMEM((rows, heads, dim), F32),
            pltpu.VMEM((rows, heads * dim), BF16),
            pltpu.SemaphoreType.DMA((out_weight.shape[0] // o_size,)),
        ],
        compiler_params=params(vmem_limit_bytes=24 << 20),
        cost_estimate=cost(2 * rows * out_weight.size, 2 * out_weight.size),
        name="project",
    )(*images, o_text, m_text, l_text, own_score, v_new, out_weight)

    others = [swap(sent, "head", j) for j in range(1, head_parts)]
    return pl.pallas_call(
        functools.partial(final_kernel, len(others)),
        out_shape=jax.ShapeDtypeStruct((rows, width // head_parts), BF16),
        in_specs=[VMEM] * (len(others) + 3),
        out_specs=VMEM,
        compiler_params=params(vmem_limit_bytes=8 << 20),
        cost_estimate=cost(8 * rows * width, 16 * rows * width),
        name="finish",
    )(*others, kept, hidden, post_gain.reshape(1, -1))


def solution(mesh):
    placed = (
        P("grp", None),
        P(),
        P(None, "head"),
        P(None, "head"),
        P(None, "head"),
        P("head", None),
        P(),
        P(),
        P("head"),
        P("grp", None, "head"),
        P("grp", None, "head"),
        P("grp"),
        P("grp", None, "head"),
        P("grp", None, "head"),
        P(),
        P(),
        P(),
    )
    return jax.shard_map(
        local, mesh=mesh, in_specs=placed, out_specs=P("grp", "head"), check_vma=False
    )
```

```python
import functools
import math

import jax
import jax.numpy as jnp
from jax import lax
from jax.experimental import pallas as pl
from jax.experimental.pallas import tpu as pltpu
from jax.sharding import PartitionSpec as P


EPS = 1e-06
NEG = -1e30
BLOCK = 128
F32 = jnp.float32
BF16 = jnp.bfloat16
HBM = pl.BlockSpec(memory_space=pltpu.HBM)
VMEM = pl.BlockSpec(memory_space=pltpu.VMEM)
SMEM = pl.BlockSpec(memory_space=pltpu.SMEM)


def cost(flops, nbytes):
    return pl.CostEstimate(flops=flops, bytes_accessed=nbytes, transcendentals=0)


def pieces_of(rows, most):
    for size in range(most, 0, -16):
        if rows % size == 0:
            return size
    return rows


def row_copies(src, dst, sems, size):
    return [
        pltpu.make_async_copy(
            src.at[pl.ds(i * size, size)], dst.at[pl.ds(i * size, size)], sems.at[i]
        )
        for i in range(src.shape[0] // size)
    ]


def rms_rope(v, gain, cosine, sine):
    mean_sq = jnp.mean(v * v, axis=-1, keepdims=True)
    v = v * lax.rsqrt(mean_sq + EPS) * gain
    return v * cosine + pltpu.roll(v, v.shape[-1] // 2, 1) * sine


def query_kernel(
    scale, size, slots, position, owner, count, hidden, gain, q_gain, freq, weight,
    q_out, normed_out, cos_out, sin_out, item, filled, w_buf, h_buf, g_buf, heads_buf, w_sem, s_sem
):
    copies = row_copies(weight, w_buf, w_sem, size)
    small = [
        pltpu.make_async_copy(hidden, h_buf, s_sem.at[0]),
        pltpu.make_async_copy(gain, g_buf, s_sem.at[1]),
    ]
    for c in small:
        c.start()
    for c in copies:
        c.start()
    me = lax.axis_index("grp")
    levels = filled.shape[0]

    def note(r, have):
        mine = owner[r] == me
        level = count[r] // BLOCK - 1
        out = []
        for n in range(levels):
            hit = mine & (level == n)
            item[n * (slots + 1) + jnp.where(hit, have[n], slots)] = r
            out.append(have[n] + hit.astype(jnp.int32))
        return tuple(out)

    have = lax.fori_loop(0, owner.shape[0], note, (jnp.int32(0),) * levels, unroll=8)
    for n in range(levels):
        filled[n] = have[n]
    rows = hidden.shape[0]
    dim = q_gain.shape[-1]
    lane = lax.broadcasted_iota(jnp.int32, (rows, dim), 1)
    row = lax.broadcasted_iota(jnp.int32, (rows, dim), 0)
    where = jnp.zeros((rows, dim), jnp.int32)
    for n in range(rows):
        where = jnp.where(row == n, position[n], where)
    angle = where.astype(F32) * freq[...]
    cosine = jnp.cos(angle)
    sine = jnp.sin(angle)
    sine = jnp.where(lane < dim // 2, -sine, sine)
    cos_out[...] = cosine
    sin_out[...] = sine
    for c in small:
        c.wait()
    h = h_buf[...].astype(F32)
    mean_sq = jnp.mean(h * h, axis=-1, keepdims=True)
    h = h * lax.rsqrt(mean_sq + EPS)
    for n in range(g_buf.shape[0]):
        part = slice(n * dim, (n + 1) * dim)
        normed_out[:, part] = (h[:, part] * g_buf[n : n + 1, :]).astype(BF16)
    acc = jnp.zeros((rows, weight.shape[1]), F32)
    for i, c in enumerate(copies):
        c.wait()
        acc = acc + jnp.dot(
            normed_out[:, i * size : (i + 1) * size],
            w_buf[i * size : (i + 1) * size, :],
            preferred_element_type=F32,
        )
    for n in range(acc.shape[1] // dim):
        v = rms_rope(acc[:, n * dim : (n + 1) * dim], q_gain[...], cosine, sine)
        heads_buf[:, n, :] = v * scale
    q_out[...] = heads_buf[...].astype(BF16)


def kv_kernel(
    size, normed, cosine, sine, k_gain, q, k_weight, v_weight, self_out, v_out,
    k_buf, vw_buf, heads_buf, k_sem, v_sem
):
    k_copies = row_copies(k_weight, k_buf, k_sem, size)
    v_copies = row_copies(v_weight, vw_buf, v_sem, size)
    for a, b in zip(k_copies, v_copies):
        a.start()
        b.start()
    k_acc = jnp.zeros((normed.shape[0], k_weight.shape[1]), F32)
    v_acc = jnp.zeros((normed.shape[0], v_weight.shape[1]), F32)
    for i, (a, b) in enumerate(zip(k_copies, v_copies)):
        x = normed[:, i * size : (i + 1) * size]
        a.wait()
        k_acc = k_acc + jnp.dot(
            x, k_buf[i * size : (i + 1) * size, :], preferred_element_type=F32
        )
        b.wait()
        v_acc = v_acc + jnp.dot(
            x, vw_buf[i * size : (i + 1) * size, :], preferred_element_type=F32
        )
    dim = k_gain.shape[-1]
    heads = q.shape[1]
    group = heads // (k_acc.shape[1] // dim)
    for n in range(heads):
        if n % group == 0:
            part = slice((n // group) * dim, (n // group + 1) * dim)
            k = rms_rope(k_acc[:, part], k_gain[...], cosine[...], sine[...])
            k = k.astype(BF16).astype(F32)
            v = v_acc[:, part].astype(BF16).astype(F32)
        heads_buf[:, n, :] = k
        v_out[:, n, :] = v
    score = jnp.sum(q[...].astype(F32) * heads_buf[...], axis=-1, keepdims=True)
    self_out[...] = jnp.broadcast_to(score, self_out.shape)


def spread(q, kv_heads):
    group = q.shape[0] // kv_heads
    owner = lax.broadcasted_iota(jnp.int32, q.shape, 0) // group
    q = q.astype(F32)
    return jnp.concatenate(
        [jnp.where(owner == n, q, 0.0) for n in range(kv_heads)], axis=1
    ).astype(BF16)


def gather_heads(o, heads, dim):
    kv_heads = o.shape[1] // dim
    owner = lax.broadcasted_iota(jnp.int32, (heads, dim), 0) // (heads // kv_heads)
    total = jnp.zeros((heads, dim), F32)
    for n in range(kv_heads):
        total = jnp.where(owner == n, o[:, n * dim : (n + 1) * dim], total)
    return total


def attend(q, keys, values, valid):
    heads, dim = q.shape
    kv_heads = keys.shape[1] // dim
    scores = lax.dot_general(
        spread(q, kv_heads), keys, (((1,), (1,)), ((), ())), preferred_element_type=F32
    )
    scores = jnp.where(valid, scores, NEG)
    top = jnp.max(scores, axis=-1, keepdims=True)
    weights = jnp.where(valid, jnp.exp(scores - top), 0.0).astype(BF16)
    total = jnp.sum(weights.astype(F32), axis=-1, keepdims=True)
    summed = jnp.dot(weights, values, preferred_element_type=F32)
    return top, total, gather_heads(summed, heads, dim)


def text_kernel(
    first, count, together, position, q, keys, values, o_out, m_out, l_out, k_buf, v_buf, k_sem, v_sem
):
    window = keys.shape[1]
    k_copies = [
        pltpu.make_async_copy(keys.at[first + i], k_buf.at[i], k_sem.at[i]) for i in range(count)
    ]
    v_copies = [
        pltpu.make_async_copy(values.at[first + i], v_buf.at[i], v_sem.at[i]) for i in range(count)
    ]
    for a, b in zip(k_copies, v_copies):
        a.start()
        b.start()
    slot = lax.broadcasted_iota(jnp.int32, (q.shape[1], window), 1)
    for base in range(0, count, together):
        part = range(base, min(base + together, count))
        for i in part:
            k_copies[i].wait()
        for i in part:
            v_copies[i].wait()
        for i in part:
            p = position[first + i]
            valid = (slot < p) & (slot != lax.rem(p, window))
            top, total, summed = attend(q[first + i], k_buf[i], v_buf[i], valid)
            o_out[i] = summed
            m_out[i] = jnp.broadcast_to(top, summed.shape)
            l_out[i] = jnp.broadcast_to(total, summed.shape)


def image_kernel(far, together, n_q, item, filled, slot, *refs):
    queries = refs[:n_q]
    (keys, values, near_out, far_out, k_buf, v_buf, q_buf, s_buf, p_buf, total_buf, stat_buf,
     k_sem, v_sem) = refs[n_q:]
    me = lax.axis_index("grp")
    slots, length, kv_width = k_buf.shape
    levels = length // BLOCK
    rows = queries[0].shape[0]
    heads, dim = queries[0].shape[1:]
    half = near_out.shape[0]
    have = [filled[n] for n in range(levels)]
    order = range(levels - 1, -1, -1)
    base, at = {}, 0
    for level in order:
        base[level] = at
        at = at + have[level]
    everything = at

    def row_of(level, n):
        return item[level * (slots + 1) + n]

    def copy_of(src, dst, sem, place, full):
        return pltpu.make_async_copy(
            src.at[place, pl.ds(0, full)], dst.at[place, pl.ds(0, full)], sem.at[place]
        )

    for src, dst, sem in ((keys, k_buf, k_sem), (values, v_buf, v_sem)):
        for level in order:
            full = (level + 1) * BLOCK

            def begin(n, carry, src=src, dst=dst, sem=sem, level=level, full=full):
                copy_of(src, dst, sem, slot[row_of(level, n)], full).start()
                return carry

            lax.fori_loop(0, have[level], begin, 0)
    near_out[...] = jnp.zeros_like(near_out)
    far_out[...] = jnp.zeros_like(far_out)
    at = 0
    for ref in queries:
        n = ref.shape[0]
        if at + n == 2 * half * rows:
            for j in range(n // rows):
                q_buf[(far ^ j) * rows : (far ^ j) * rows + rows] = ref[j * rows : j * rows + rows]
        else:
            q_buf[at : at + n] = ref[...]
        at += n

    def target(r):
        return lax.bitwise_xor(r // rows, me), lax.rem(r, rows)

    def steps(level):
        return (have[level] + together - 1) // together

    def todo(level, step):
        found = []
        for u in range(together):
            n = step * together + u
            live = n < have[level]
            r = row_of(level, jnp.where(live, n, 0))
            found.append((live, jnp.where(live, base[level] + n, slots), r, slot[r]))
        return found

    for level in order:
        full = (level + 1) * BLOCK

        def score(step, carry, level=level, full=full):
            found = todo(level, step)
            for live, _, _, place in found:
                @pl.when(live)
                def _():
                    copy_of(keys, k_buf, k_sem, place, full).wait()
            for _, put, r, place in found:
                group, lane = target(r)
                q = spread(q_buf[group * rows + lane], kv_width // dim)
                s_buf[put, :, :full] = lax.dot_general(
                    q, k_buf[place, :full, :], (((1,), (1,)), ((), ())), preferred_element_type=F32
                )
                if full < length:
                    s_buf[put, :, full:] = jnp.full((heads, length - full), NEG, F32)
            return carry

        lax.fori_loop(0, steps(level), score, 0)

    lane_of = lax.broadcasted_iota(jnp.int32, (1, heads, dim), 2)

    def soften(step, carry):
        part = pl.ds(step * 8, 8)
        scores = s_buf[part]
        top = jnp.max(scores, axis=-1, keepdims=True)
        weights = jnp.exp(scores - top).astype(BF16)
        p_buf[part] = weights
        total = jnp.sum(weights.astype(F32), axis=-1, keepdims=True)
        total_buf[part] = jnp.broadcast_to(total, (8, heads, dim))
        level_sum = top + jnp.log(total)
        high = level_sum.astype(BF16).astype(F32)
        middle = (level_sum - high).astype(BF16).astype(F32)
        low = level_sum - high - middle
        kind = lax.rem(lane_of, 3)
        stat_buf[part] = jnp.where(kind == 0, high, jnp.where(kind == 1, middle, low))
        return carry

    lax.fori_loop(0, (everything + 7) // 8, soften, 0)

    for level in order:
        full = (level + 1) * BLOCK

        def weigh(step, carry, level=level, full=full):
            found = todo(level, step)
            for live, _, _, place in found:
                @pl.when(live)
                def _():
                    copy_of(values, v_buf, v_sem, place, full).wait()
            done = []
            for live, put, r, place in found:
                summed = jnp.dot(
                    p_buf[put, :, :full], v_buf[place, :full, :], preferred_element_type=F32
                )
                mean = gather_heads(summed, heads, dim) / total_buf[put]
                group, lane = target(r)
                at_lane = lane_of[0] - 3 * lane
                stats = jnp.where((at_lane >= 0) & (at_lane < 3), stat_buf[put], 0.0)
                done.append((live, group, lane, mean.astype(BF16), stats))
            for live, group, lane, mean, stats in done:
                is_near = group < half
                for keep, ref, at in (
                    (is_near, near_out, group),
                    (jnp.logical_not(is_near), far_out, lax.bitwise_xor(group, far)),
                ):
                    @pl.when(live & keep)
                    def _():
                        ref[at, lane] = mean
                        ref[at, rows] = (ref[at, rows].astype(F32) + stats).astype(BF16)
            return carry

        lax.fori_loop(0, steps(level), weigh, 0)


def out_kernel(size, n_image, *refs):
    images = [ref.at[0] for ref in refs[:n_image]]
    o_text, m_text, l_text, own, v_new, weight, sent, kept, heads_buf, at_buf = refs[n_image:]
    rows, heads, dim = o_text.shape
    stats = images[0][rows].astype(F32)
    for ref in images[1:]:
        stats = stats + ref[rows].astype(F32)
    for r in range(rows):
        mean = images[0][r].astype(F32)
        for ref in images[1:]:
            mean = mean + ref[r].astype(F32)
        image_level = (
            stats[:, 3 * r : 3 * r + 1] + stats[:, 3 * r + 1 : 3 * r + 2]
        ) + stats[:, 3 * r + 2 : 3 * r + 3]
        m = m_text[r]
        s = own[r]
        top = jnp.maximum(jnp.maximum(image_level, m), s)
        e_image = jnp.exp(image_level - top)
        e_text = jnp.exp(m - top)
        e_own = jnp.exp(s - top)
        upper = mean * e_image + o_text[r] * e_text + v_new[r] * e_own
        lower = e_image + l_text[r] * e_text + e_own
        heads_buf[r] = upper / lower
    for n in range(heads):
        at_buf[:, n * dim : (n + 1) * dim] = heads_buf[:, n, :].astype(BF16)
    for i in range(weight.shape[0] // size):
        part = jnp.dot(
            at_buf[:, i * size : (i + 1) * size],
            weight[i * size : (i + 1) * size, :],
            preferred_element_type=F32,
        )
        if i == 0:
            kept[...] = part
        else:
            kept[...] += part
    sent[...] = kept[...].astype(BF16)


def final_kernel(n_others, *refs):
    others = refs[:n_others]
    kept, hidden, gain, out = refs[n_others:]
    y = kept[...]
    for ref in others:
        y = y + ref[...].astype(F32)
    mean_sq = jnp.sum(y * y, axis=-1, keepdims=True) / y.shape[1]
    scale = lax.rsqrt(mean_sq + EPS)
    width = out.shape[1]
    me = lax.axis_index("head")
    for n in range(y.shape[1] // width):
        @pl.when(me == n)
        def _():
            part = slice(n * width, (n + 1) * width)
            out[...] = (hidden[:, part].astype(F32) + y[:, part] * scale * gain[...]).astype(BF16)


def swap(x, axis, k):
    n = lax.axis_size(axis)
    return lax.ppermute(x, axis, [(i, i ^ k) for i in range(n)])


def body(
    hidden, pre_gain, query_weight, key_weight, value_weight, out_weight, query_norm_gain, key_gain,
    post_gain, text_keys, text_values, text_position, image_keys, image_values, image_owner,
    image_slot, image_count,
):
    rows, width = hidden.shape
    dim = query_norm_gain.shape[0]
    heads = query_weight.shape[1] // dim
    kv_width = key_weight.shape[1]
    groups = lax.axis_size("grp")
    head_parts = lax.axis_size("head")
    slots, length = image_keys.shape[0], image_keys.shape[1]
    levels = length // BLOCK
    scale = 1.0 / math.sqrt(width // (heads * head_parts))
    half = dim // 2
    freq = jnp.exp(-jnp.log(1000000.0) * jnp.arange(half, dtype=F32) / half)
    freq = jnp.concatenate([freq, freq])[None, :]

    size = pieces_of(width, 768)
    n_copies = width // size
    q, normed, cosine, sine, item, filled = pl.pallas_call(
        functools.partial(query_kernel, scale, size, slots),
        out_shape=(
            jax.ShapeDtypeStruct((rows, heads, dim), BF16),
            jax.ShapeDtypeStruct((rows, width), BF16),
            jax.ShapeDtypeStruct((rows, dim), F32),
            jax.ShapeDtypeStruct((rows, dim), F32),
            jax.ShapeDtypeStruct((levels * (slots + 1),), jnp.int32),
            jax.ShapeDtypeStruct((levels,), jnp.int32),
        ),
        in_specs=[SMEM, SMEM, SMEM, HBM, HBM, VMEM, VMEM, HBM],
        out_specs=(VMEM, VMEM, VMEM, VMEM, SMEM, SMEM),
        scratch_shapes=[
            pltpu.VMEM(query_weight.shape, BF16),
            pltpu.VMEM(hidden.shape, BF16),
            pltpu.VMEM((width // dim, dim), F32),
            pltpu.VMEM((rows, heads, dim), F32),
            pltpu.SemaphoreType.DMA((n_copies,)),
            pltpu.SemaphoreType.DMA((2,)),
        ],
        compiler_params=pltpu.CompilerParams(vmem_limit_bytes=16 << 20),
        cost_estimate=cost(2 * rows * query_weight.size, 2 * query_weight.size),
        name="query",
    )(
        text_position, image_owner, image_count, hidden, pre_gain.reshape(-1, dim),
        query_norm_gain.reshape(1, -1), freq, query_weight,
    )

    far = groups // 2 + groups // 4 if groups > 4 else groups // 2
    queries = [q]
    held = q
    k = 1
    while k < groups:
        got = swap(held, "grp", far if 2 * k == groups else k)
        queries.append(got)
        k *= 2
        if k < groups:
            held = jnp.concatenate([held, got], axis=0)

    own_score, v_new = pl.pallas_call(
        functools.partial(kv_kernel, size),
        out_shape=(jax.ShapeDtypeStruct((rows, heads, dim), F32),) * 2,
        in_specs=[VMEM, VMEM, VMEM, VMEM, VMEM, HBM, HBM],
        out_specs=(VMEM, VMEM),
        scratch_shapes=[
            pltpu.VMEM(key_weight.shape, BF16),
            pltpu.VMEM(value_weight.shape, BF16),
            pltpu.VMEM((rows, heads, dim), F32),
            pltpu.SemaphoreType.DMA((n_copies,)),
            pltpu.SemaphoreType.DMA((n_copies,)),
        ],
        compiler_params=pltpu.CompilerParams(vmem_limit_bytes=16 << 20),
        cost_estimate=cost(4 * rows * key_weight.size, 4 * key_weight.size),
        name="keyvalue",
    )(normed, cosine, sine, key_gain.reshape(1, -1), q, key_weight, value_weight)

    window = text_keys.shape[1]
    o_text, m_text, l_text = pl.pallas_call(
        functools.partial(text_kernel, 0, rows, 4),
        out_shape=(jax.ShapeDtypeStruct((rows, heads, dim), F32),) * 3,
        in_specs=[SMEM, VMEM, HBM, HBM],
        out_specs=(VMEM,) * 3,
        scratch_shapes=[
            pltpu.VMEM((rows, window, kv_width), BF16),
            pltpu.VMEM((rows, window, kv_width), BF16),
            pltpu.SemaphoreType.DMA((rows,)),
            pltpu.SemaphoreType.DMA((rows,)),
        ],
        compiler_params=pltpu.CompilerParams(vmem_limit_bytes=22 << 20),
        cost_estimate=cost(8 * heads * text_keys.size, 4 * text_keys.size),
        name="text",
    )(text_position, q, text_keys, text_values)

    near, other = pl.pallas_call(
        functools.partial(image_kernel, far, 4, len(queries)),
        out_shape=(jax.ShapeDtypeStruct((groups // 2, rows + 1, heads, dim), BF16),) * 2,
        in_specs=[SMEM] * 3 + [VMEM] * len(queries) + [HBM, HBM],
        out_specs=(VMEM, VMEM),
        scratch_shapes=[
            pltpu.VMEM(image_keys.shape, BF16),
            pltpu.VMEM(image_keys.shape, BF16),
            pltpu.VMEM((groups * rows, heads, dim), BF16),
            pltpu.VMEM((slots + 8, heads, length), F32),
            pltpu.VMEM((slots + 8, heads, length), BF16),
            pltpu.VMEM((slots + 8, heads, dim), F32),
            pltpu.VMEM((slots + 8, heads, dim), F32),
            pltpu.SemaphoreType.DMA((slots,)),
            pltpu.SemaphoreType.DMA((slots,)),
        ],
        compiler_params=pltpu.CompilerParams(vmem_limit_bytes=18 << 20),
        cost_estimate=cost(8 * heads * image_keys.size, 4 * image_keys.size),
        name="image",
    )(item, filled, image_slot, *queries, image_keys, image_values)

    images = [near]
    moved, k = other, groups // 2
    while k:
        images.append(swap(moved, "grp", far if 2 * k == groups else k))
        k //= 2
        if k:
            moved = sum(x[k : 2 * k] for x in images)

    o_size = pieces_of(out_weight.shape[0], 256)
    sent, kept = pl.pallas_call(
        functools.partial(out_kernel, o_size, len(images)),
        out_shape=(
            jax.ShapeDtypeStruct((rows, width), BF16),
            jax.ShapeDtypeStruct((rows, width), F32),
        ),
        in_specs=[VMEM] * (len(images) + 6),
        out_specs=(VMEM, VMEM),
        scratch_shapes=[pltpu.VMEM((rows, heads, dim), F32), pltpu.VMEM((rows, heads * dim), BF16)],
        compiler_params=pltpu.CompilerParams(vmem_limit_bytes=8 << 20),
        cost_estimate=cost(2 * rows * out_weight.size, 2 * out_weight.size),
        name="project",
    )(*images, o_text, m_text, l_text, own_score, v_new, out_weight)

    others = [swap(sent, "head", j) for j in range(1, head_parts)]
    return pl.pallas_call(
        functools.partial(final_kernel, len(others)),
        out_shape=jax.ShapeDtypeStruct((rows, width // head_parts), BF16),
        in_specs=[VMEM] * (len(others) + 3),
        out_specs=VMEM,
        compiler_params=pltpu.CompilerParams(vmem_limit_bytes=8 << 20),
        cost_estimate=cost(8 * rows * width, 16 * rows * width),
        name="finish",
    )(*others, kept, hidden, post_gain.reshape(1, -1))


def solution(mesh):
    placed = (
        P("grp", None),
        P(),
        P(None, "head"),
        P(None, "head"),
        P(None, "head"),
        P("head", None),
        P(),
        P(),
        P("head"),
        P("grp", None, "head"),
        P("grp", None, "head"),
        P("grp"),
        P("grp", None, "head"),
        P("grp", None, "head"),
        P(),
        P(),
        P(),
    )
    return jax.shard_map(
        body, mesh=mesh, in_specs=placed, out_specs=P("grp", "head"), check_vma=False
    )
```

```python
import functools
import math

import jax
import jax.numpy as jnp
from jax import lax
from jax.experimental import pallas as pl
from jax.experimental.pallas import tpu as pltpu
from jax.sharding import PartitionSpec as P


EPS = 1e-06
NEG = -1e30
SMALL = 4 << 20
F32 = jnp.float32
BF16 = jnp.bfloat16
HBM = pl.BlockSpec(memory_space=pltpu.HBM)
VMEM = pl.BlockSpec(memory_space=pltpu.VMEM)
SMEM = pl.BlockSpec(memory_space=pltpu.SMEM)


def cost(flops, nbytes):
    return pl.CostEstimate(flops=flops, bytes_accessed=nbytes, transcendentals=0)


def pieces_of(rows, most):
    for size in range(most, 0, -16):
        if rows % size == 0:
            return size
    return rows


def row_copies(src, dst, sems, size):
    return [
        pltpu.make_async_copy(
            src.at[pl.ds(i * size, size)], dst.at[pl.ds(i * size, size)], sems.at[i]
        )
        for i in range(src.shape[0] // size)
    ]


def rms_rope(v, gain, cosine, sine):
    mean_sq = jnp.mean(v * v, axis=-1, keepdims=True)
    v = v * lax.rsqrt(mean_sq + EPS) * gain
    return v * cosine + pltpu.roll(v, v.shape[-1] // 2, 1) * sine


def query_kernel(
    scale, size, freq, hidden, gain, q_gain_in, k_gain, position_in, owner, count, slot, weight,
    q_out, normed_out, cos_out, sin_out, k_gain_out, position, owner_out, count_out, slot_out,
    w_buf, h_buf, g_buf, q_gain, heads_buf, w_sem, s_sem
):
    copies = row_copies(weight, w_buf, w_sem, size)
    pairs = (
        (hidden, h_buf), (gain, g_buf), (position_in, position), (q_gain_in, q_gain),
        (k_gain, k_gain_out), (owner, owner_out), (count, count_out), (slot, slot_out),
    )
    small = [pltpu.make_async_copy(a, b, s_sem.at[i]) for i, (a, b) in enumerate(pairs)]
    for c in small[:2] + copies[:1] + small[2:] + copies[1:]:
        c.start()
    rows = hidden.shape[0]
    dim = q_gain.shape[-1]
    for c in small[:2]:
        c.wait()
    h = h_buf[...].astype(F32)
    mean_sq = jnp.mean(h * h, axis=-1, keepdims=True)
    h = h * lax.rsqrt(mean_sq + EPS)
    for n in range(g_buf.shape[0]):
        part = slice(n * dim, (n + 1) * dim)
        normed_out[:, part] = (h[:, part] * g_buf[n : n + 1, :]).astype(BF16)
    acc = jnp.zeros((rows, weight.shape[1]), F32)
    for i, c in enumerate(copies):
        c.wait()
        acc = acc + jnp.dot(
            normed_out[:, i * size : (i + 1) * size],
            w_buf[i * size : (i + 1) * size, :],
            preferred_element_type=F32,
        )
        if i == 0:
            small[2].wait()
            lane = lax.broadcasted_iota(jnp.int32, (rows, dim), 1)
            row = lax.broadcasted_iota(jnp.int32, (rows, dim), 0)
            where = jnp.zeros((rows, dim), jnp.int32)
            for n in range(rows):
                where = jnp.where(row == n, position[n], where)
            angle = where.astype(F32) * freq[...]
            cosine = jnp.cos(angle)
            sine = jnp.sin(angle)
            sine = jnp.where(lane < dim // 2, -sine, sine)
            cos_out[...] = cosine
            sin_out[...] = sine
    for c in small[3:]:
        c.wait()
    cosine, sine = cos_out[...], sin_out[...]
    for n in range(acc.shape[1] // dim):
        v = rms_rope(acc[:, n * dim : (n + 1) * dim], q_gain[...], cosine, sine)
        heads_buf[:, n, :] = v * scale
    q_out[...] = heads_buf[...].astype(BF16)


def kv_kernel(normed, cosine, sine, k_gain, q, k_weight, v_weight, self_out, v_out, heads_buf):
    k_acc = jnp.dot(normed[...], k_weight[...], preferred_element_type=F32)
    v_acc = jnp.dot(normed[...], v_weight[...], preferred_element_type=F32)
    dim = k_gain.shape[-1]
    heads = q.shape[1]
    group = heads // (k_acc.shape[1] // dim)
    for n in range(heads):
        if n % group == 0:
            part = slice((n // group) * dim, (n // group + 1) * dim)
            k = rms_rope(k_acc[:, part], k_gain[...], cosine[...], sine[...])
            k = k.astype(BF16).astype(F32)
            v = v_acc[:, part].astype(BF16).astype(F32)
        heads_buf[:, n, :] = k
        v_out[:, n, :] = v
    score = jnp.sum(q[...].astype(F32) * heads_buf[...], axis=-1, keepdims=True)
    self_out[...] = jnp.broadcast_to(score, self_out.shape)


def text_parts(rows):
    return ((0, rows // 2), (rows // 2, rows))


def spread(q, kv_heads):
    group = q.shape[0] // kv_heads
    owner = lax.broadcasted_iota(jnp.int32, q.shape, 0) // group
    q = q.astype(F32)
    return jnp.concatenate(
        [jnp.where(owner == n, q, 0.0) for n in range(kv_heads)], axis=1
    ).astype(BF16)


def gather_heads(o, heads, dim):
    kv_heads = o.shape[1] // dim
    owner = lax.broadcasted_iota(jnp.int32, (heads, dim), 0) // (heads // kv_heads)
    total = jnp.zeros((heads, dim), F32)
    for n in range(kv_heads):
        total = jnp.where(owner == n, o[:, n * dim : (n + 1) * dim], total)
    return total


def score_block(q, keys, valid):
    scores = lax.dot_general(
        spread(q, keys.shape[1] // q.shape[1]), keys, (((1,), (1,)), ((), ())),
        preferred_element_type=F32,
    )
    return jnp.where(valid, scores, NEG)


def weigh_block(scores, values, heads, dim):
    top = jnp.max(scores, axis=-1, keepdims=True)
    weights = jnp.exp(scores - top).astype(BF16)
    total = jnp.sum(weights.astype(F32), axis=-1, keepdims=True)
    summed = jnp.dot(weights, values, preferred_element_type=F32)
    return top, total, gather_heads(summed, heads, dim)


def plan(slots, owner, count, slot, item, length, filled):
    me = lax.axis_index("grp")

    def note(r, have):
        hit = owner[r] == me
        at = jnp.where(hit, have, slots)
        item[at] = r * slots + slot[r]
        length[at] = count[r]
        return have + hit.astype(jnp.int32)

    filled[0] = lax.fori_loop(0, owner.shape[0], note, jnp.int32(0), unroll=8)


def text_kernel(first, slots, position, q, *refs):
    if slots:
        owner, count_in, slot_in = refs[:3]
        keys, values, o_out, m_out, l_out, item, length, filled = refs[3:11]
        k_buf, v_buf, k_sem, v_sem = refs[11:]
    else:
        keys, values, o_out, m_out, l_out, k_buf, v_buf, k_sem, v_sem = refs
    count, window, _ = k_buf.shape
    heads, dim = q.shape[1:]
    copies = [
        [
            pltpu.make_async_copy(src.at[first + i], dst.at[i], sem.at[i])
            for src, dst, sem in ((keys, k_buf, k_sem), (values, v_buf, v_sem))
        ]
        for i in range(count)
    ]
    for pair in copies:
        for c in pair:
            c.start()
    if slots:
        plan(slots, owner, count_in, slot_in, item, length, filled)
    column = lax.broadcasted_iota(jnp.int32, (heads, window), 1)

    def score(i):
        p = position[first + i]
        valid = (column < p) & (column != lax.rem(p, window))
        return score_block(q[first + i], k_buf[i], valid)

    copies[0][0].wait()
    scores = score(0)
    for i in range(count):
        if i + 1 < count:
            copies[i + 1][0].wait()
        copies[i][1].wait()
        later = score(i + 1) if i + 1 < count else None
        top, total, summed = weigh_block(scores, v_buf[i], heads, dim)
        o_out[i] = summed
        m_out[i] = jnp.broadcast_to(top, summed.shape)
        l_out[i] = jnp.broadcast_to(total, summed.shape)
        scores = later


def image_kernel(batch, n_q, item, tokens, filled, *refs):
    queries = refs[:n_q]
    keys, values, mine, other, q_buf, s_buf, out_buf = refs[n_q:]
    me = lax.axis_index("grp")
    slots, length, _ = keys.shape
    rows = queries[0].shape[0]
    heads, dim = queries[0].shape[1:]
    half = mine.shape[0]
    have = filled[0]
    out_buf[...] = jnp.zeros_like(out_buf)
    known, step = [0], half
    q_buf[:rows] = queries[0][...]
    for ref in queries[1:]:
        new = [j ^ step for j in known]
        step //= 2
        for n, j in enumerate(new):
            q_buf[j * rows : (j + 1) * rows] = ref[n * rows : (n + 1) * rows]
        known = known + new
    column = lax.broadcasted_iota(jnp.int32, (heads, length), 1)
    lane_of = lax.broadcasted_iota(jnp.int32, (heads, dim), 1)

    def members(t):
        found = []
        for u in range(batch):
            n = t * batch + u
            live = n < have
            n = jnp.minimum(n, have - 1)
            r = item[n] // slots
            found.append((n, live, r, item[n] - r * slots))
        return found

    def score(t):
        for u, (n, live, r, place) in enumerate(members(t)):
            group, lane = lax.bitwise_xor(r // rows, me), lax.rem(r, rows)
            s_buf[lax.rem(t, 2), u] = score_block(
                q_buf[group * rows + lane], keys[place], column < tokens[n]
            )

    def weigh(t):
        done = []
        for u, (n, live, r, place) in enumerate(members(t)):
            top, total, summed = weigh_block(s_buf[lax.rem(t, 2), u], values[place], heads, dim)
            mean = (summed / total).astype(BF16)
            group, lane = lax.bitwise_xor(r // rows, me), lax.rem(r, rows)
            level = top + jnp.log(total)
            high = level.astype(BF16).astype(F32)
            middle = (level - high).astype(BF16).astype(F32)
            low = level - high - middle
            kind = lane_of - 3 * lane
            stats = jnp.where(
                kind == 0, high, jnp.where(kind == 1, middle, jnp.where(kind == 2, low, 0.0))
            )
            at = jnp.where(live, group, 2 * half) * (rows + 1)
            done.append((at + lane, at + rows, mean, stats))
        for at, stats_at, mean, stats in done:
            out_buf[at] = mean
            out_buf[stats_at] = (out_buf[stats_at].astype(F32) + stats).astype(BF16)

    last = (have + batch - 1) // batch - 1

    @pl.when(have > 0)
    def _():
        score(0)

        def both(t, carry):
            score(t + 1)
            weigh(t)
            return carry

        lax.fori_loop(0, last, both, 0)
        weigh(last)

    for j in range(half):
        for n in range(rows + 1):
            mine[j, n] = out_buf[2 * j * (rows + 1) + n]
            other[j, n] = out_buf[(2 * j + 1) * (rows + 1) + n]


def out_kernel(size, n_image, n_text, *refs):
    images = refs[:n_image]
    text = refs[n_image : n_image + n_text]
    own, v_new, weight, sent, kept, heads_buf, at_buf = refs[n_image + n_text :]
    rows, heads, dim = own.shape
    holds = [(n, i) for n in range(0, n_text, 3) for i in range(text[n].shape[0])]
    stats = images[0][rows].astype(F32)
    for ref in images[1:]:
        stats = stats + ref[rows].astype(F32)
    for r in range(rows):
        mean = images[0][r].astype(F32)
        for ref in images[1:]:
            mean = mean + ref[r].astype(F32)
        image_level = (
            stats[:, 3 * r : 3 * r + 1] + stats[:, 3 * r + 1 : 3 * r + 2]
        ) + stats[:, 3 * r + 2 : 3 * r + 3]
        part, at = holds[r]
        o_text, m, l_text = (ref[at] for ref in text[part : part + 3])
        s = own[r]
        top = jnp.maximum(jnp.maximum(image_level, m), s)
        e_image = jnp.exp(image_level - top)
        e_text = jnp.exp(m - top)
        e_own = jnp.exp(s - top)
        upper = mean * e_image + o_text * e_text + v_new[r] * e_own
        lower = e_image + l_text * e_text + e_own
        heads_buf[r] = upper / lower
    for n in range(heads):
        at_buf[:, n * dim : (n + 1) * dim] = heads_buf[:, n, :].astype(BF16)
    for i in range(weight.shape[0] // size):
        part = jnp.dot(
            at_buf[:, i * size : (i + 1) * size],
            weight[i * size : (i + 1) * size, :],
            preferred_element_type=F32,
        )
        if i == 0:
            kept[...] = part
        else:
            kept[...] += part
    sent[...] = kept[...].astype(BF16)


def final_kernel(n_others, *refs):
    others = refs[:n_others]
    kept, hidden, gain, out = refs[n_others:]
    y = kept[...]
    for ref in others:
        y = y + ref[...].astype(F32)
    mean_sq = jnp.sum(y * y, axis=-1, keepdims=True) / y.shape[1]
    scale = lax.rsqrt(mean_sq + EPS)
    width = out.shape[1]
    me = lax.axis_index("head")
    for n in range(y.shape[1] // width):
        @pl.when(me == n)
        def _():
            part = slice(n * width, (n + 1) * width)
            out[...] = (hidden[:, part].astype(F32) + y[:, part] * scale * gain[...]).astype(BF16)


def stay(x):
    return pltpu.with_memory_space_constraint(x, pltpu.HBM)


def swap(x, axis, k):
    n = lax.axis_size(axis)
    return lax.ppermute(x, axis, [(i, i ^ k) for i in range(n)])


def body(
    hidden, pre_gain, query_weight, key_weight, value_weight, out_weight, query_norm_gain, key_gain,
    post_gain, text_keys, text_values, text_position, image_keys, image_values, image_owner,
    image_slot, image_count,
):
    rows, width = hidden.shape
    dim = query_norm_gain.shape[0]
    heads = query_weight.shape[1] // dim
    groups = lax.axis_size("grp")
    head_parts = lax.axis_size("head")
    slots, length = image_keys.shape[0], image_keys.shape[1]
    scale = 1.0 / math.sqrt(width // (heads * head_parts))
    half = dim // 2
    freq = jnp.exp(-jnp.log(1000000.0) * jnp.arange(half, dtype=F32) / half)
    freq = jnp.concatenate([freq, freq])[None, :]

    size = pieces_of(width, 768)
    n_copies = width // size
    whole = jax.ShapeDtypeStruct(image_owner.shape, jnp.int32)
    q, normed, cosine, sine, k_gain, position, owner, count, slot = pl.pallas_call(
        functools.partial(query_kernel, scale, size),
        out_shape=(
            jax.ShapeDtypeStruct((rows, heads, dim), BF16),
            jax.ShapeDtypeStruct((rows, width), BF16),
            jax.ShapeDtypeStruct((rows, dim), F32),
            jax.ShapeDtypeStruct((rows, dim), F32),
            jax.ShapeDtypeStruct((1, dim), F32),
            jax.ShapeDtypeStruct((rows,), jnp.int32),
            whole, whole, whole,
        ),
        in_specs=[VMEM] + [HBM] * 9,
        out_specs=(VMEM,) * 5 + (SMEM,) * 4,
        scratch_shapes=[
            pltpu.VMEM(query_weight.shape, BF16),
            pltpu.VMEM(hidden.shape, BF16),
            pltpu.VMEM((width // dim, dim), F32),
            pltpu.VMEM((1, dim), F32),
            pltpu.VMEM((rows, heads, dim), F32),
            pltpu.SemaphoreType.DMA((n_copies,)),
            pltpu.SemaphoreType.DMA((8,)),
        ],
        compiler_params=pltpu.CompilerParams(vmem_limit_bytes=16 << 20),
        cost_estimate=cost(2 * rows * query_weight.size, 2 * query_weight.size),
        name="query",
    )(
        freq,
        *map(
            stay,
            (
                hidden, pre_gain.reshape(-1, dim), query_norm_gain.reshape(1, -1),
                key_gain.reshape(1, -1), text_position, image_owner, image_count, image_slot,
                query_weight,
            ),
        ),
    )

    queries = [q]
    held = q
    k = groups // 2
    while k:
        got = swap(held, "grp", k)
        queries.append(got)
        k //= 2
        if k:
            held = jnp.concatenate([held, got], axis=0)

    text = []
    for n, (first, last) in enumerate(text_parts(rows)):
        part = (last - first,) + text_keys.shape[1:]
        share = math.prod(part)
        lead = n == 0
        got = pl.pallas_call(
            functools.partial(text_kernel, first, slots if lead else 0),
            out_shape=(jax.ShapeDtypeStruct((last - first, heads, dim), F32),) * 3
            + lead * (
                jax.ShapeDtypeStruct((slots + 1,), jnp.int32),
                jax.ShapeDtypeStruct((slots + 1,), jnp.int32),
                jax.ShapeDtypeStruct((1,), jnp.int32),
            ),
            in_specs=[SMEM, VMEM] + lead * [SMEM] * 3 + [HBM, HBM],
            out_specs=(VMEM,) * 3 + lead * (SMEM,) * 3,
            scratch_shapes=[
                pltpu.VMEM(part, BF16),
                pltpu.VMEM(part, BF16),
                pltpu.SemaphoreType.DMA(part[:1]),
                pltpu.SemaphoreType.DMA(part[:1]),
            ],
            compiler_params=pltpu.CompilerParams(vmem_limit_bytes=4 * share + SMALL),
            cost_estimate=cost(8 * heads * share, 4 * share),
        )(position, q, *(lead * (owner, count, slot)), stay(text_keys), stay(text_values))
        text += got[:3]
        if lead:
            items = got[3:]

    batch = 8
    mine, other = pl.pallas_call(
        functools.partial(image_kernel, batch, len(queries)),
        out_shape=(jax.ShapeDtypeStruct((groups // 2, rows + 1, heads, dim), BF16),) * 2,
        in_specs=[SMEM] * 3 + [VMEM] * (len(queries) + 2),
        out_specs=(VMEM, VMEM),
        scratch_shapes=[
            pltpu.VMEM((groups * rows, heads, dim), BF16),
            pltpu.VMEM((2, batch, heads, length), F32),
            pltpu.VMEM(((groups + 1) * (rows + 1), heads, dim), BF16),
        ],
        compiler_params=pltpu.CompilerParams(vmem_limit_bytes=SMALL),
        cost_estimate=cost(8 * heads * image_keys.size, 4 * image_keys.size),
        name="image",
    )(*items, *queries, image_keys, image_values)

    key_weight, value_weight, out_weight, mine, other = lax.optimization_barrier(
        (key_weight, value_weight, out_weight, mine, other)
    )
    own_score, v_new = pl.pallas_call(
        kv_kernel,
        out_shape=(jax.ShapeDtypeStruct((rows, heads, dim), F32),) * 2,
        in_specs=[VMEM] * 7,
        out_specs=(VMEM, VMEM),
        scratch_shapes=[pltpu.VMEM((rows, heads, dim), F32)],
        compiler_params=pltpu.CompilerParams(vmem_limit_bytes=SMALL),
        cost_estimate=cost(4 * rows * key_weight.size, 4 * key_weight.size),
        name="keyvalue",
    )(normed, cosine, sine, k_gain, q, key_weight, value_weight)

    got = swap(other, "grp", 1)
    images = []
    for j in range(groups // 2):
        moved = mine[j] + got[j]
        images.append(swap(moved, "grp", 2 * j) if j else moved)

    o_size = pieces_of(out_weight.shape[0], 256)
    sent, kept = pl.pallas_call(
        functools.partial(out_kernel, o_size, len(images), len(text)),
        out_shape=(
            jax.ShapeDtypeStruct((rows, width), BF16),
            jax.ShapeDtypeStruct((rows, width), F32),
        ),
        in_specs=[VMEM] * (len(images) + len(text) + 3),
        out_specs=(VMEM, VMEM),
        scratch_shapes=[pltpu.VMEM((rows, heads, dim), F32), pltpu.VMEM((rows, heads * dim), BF16)],
        compiler_params=pltpu.CompilerParams(vmem_limit_bytes=SMALL),
        cost_estimate=cost(2 * rows * out_weight.size, 2 * out_weight.size),
        name="project",
    )(*images, *text, own_score, v_new, out_weight)

    others = [swap(sent, "head", j) for j in range(1, head_parts)]
    return pl.pallas_call(
        functools.partial(final_kernel, len(others)),
        out_shape=jax.ShapeDtypeStruct((rows, width // head_parts), BF16),
        in_specs=[VMEM] * (len(others) + 3),
        out_specs=VMEM,
        compiler_params=pltpu.CompilerParams(vmem_limit_bytes=SMALL),
        cost_estimate=cost(8 * rows * width, 16 * rows * width),
        name="finish",
    )(*others, kept, hidden, post_gain.reshape(1, -1))


def solution(mesh):
    placed = (
        P("grp", None),
        P(),
        P(None, "head"),
        P(None, "head"),
        P(None, "head"),
        P("head", None),
        P(),
        P(),
        P("head"),
        P("grp", None, "head"),
        P("grp", None, "head"),
        P("grp"),
        P("grp", None, "head"),
        P("grp", None, "head"),
        P(),
        P(),
        P(),
    )
    return jax.shard_map(
        body, mesh=mesh, in_specs=placed, out_specs=P("grp", "head"), check_vma=False
    )
```

```python
import functools
import math

import jax
import jax.numpy as jnp
from jax import lax
from jax.experimental import pallas as pl
from jax.experimental.pallas import tpu as pltpu
from jax.sharding import PartitionSpec as P


EPS = 1e-06
NEG = -1e30
BLOCK = 128
SMALL = 4 << 20
SIZES = 64
F32 = jnp.float32
BF16 = jnp.bfloat16
HBM = pl.BlockSpec(memory_space=pltpu.HBM)
VMEM = pl.BlockSpec(memory_space=pltpu.VMEM)
SMEM = pl.BlockSpec(memory_space=pltpu.SMEM)


def cost(flops, nbytes):
    return pl.CostEstimate(flops=flops, bytes_accessed=nbytes, transcendentals=0)


def pieces_of(rows, most):
    for size in range(most, 0, -16):
        if rows % size == 0:
            return size
    return rows


def row_copies(src, dst, sems, size):
    return [
        pltpu.make_async_copy(
            src.at[pl.ds(i * size, size)], dst.at[pl.ds(i * size, size)], sems.at[i]
        )
        for i in range(src.shape[0] // size)
    ]


def rms_rope(v, gain, cosine, sine):
    mean_sq = jnp.mean(v * v, axis=-1, keepdims=True)
    v = v * lax.rsqrt(mean_sq + EPS) * gain
    return v * cosine + pltpu.roll(v, v.shape[-1] // 2, 1) * sine


def query_kernel(
    scale, size, slots, freq, hidden, gain, q_gain_in, k_gain, position_in, owner, count, slot, weight,
    q_out, normed_out, cos_out, sin_out, k_gain_out, codes,
    w_buf, h_buf, g_buf, q_gain, heads_buf, position, owner_buf, count_buf, slot_buf, w_sem, s_sem
):
    copies = row_copies(weight, w_buf, w_sem, size)
    pairs = (
        (hidden, h_buf), (gain, g_buf), (position_in, position), (q_gain_in, q_gain),
        (k_gain, k_gain_out),
        (owner, owner_buf), (count, count_buf), (slot, slot_buf),
    )
    small = [pltpu.make_async_copy(a, b, s_sem.at[i]) for i, (a, b) in enumerate(pairs)]
    for c in small[:2] + copies[:1] + small[2:] + copies[1:]:
        c.start()
    rows = hidden.shape[0]
    dim = q_gain.shape[-1]
    for c in small[:2]:
        c.wait()
    h = h_buf[...].astype(F32)
    mean_sq = jnp.mean(h * h, axis=-1, keepdims=True)
    h = h * lax.rsqrt(mean_sq + EPS)
    for n in range(g_buf.shape[0]):
        part = slice(n * dim, (n + 1) * dim)
        normed_out[:, part] = (h[:, part] * g_buf[n : n + 1, :]).astype(BF16)
    acc = jnp.zeros((rows, weight.shape[1]), F32)
    for i, c in enumerate(copies):
        c.wait()
        acc = acc + jnp.dot(
            normed_out[:, i * size : (i + 1) * size],
            w_buf[i * size : (i + 1) * size, :],
            preferred_element_type=F32,
        )
        if i == 0:
            small[2].wait()
            lane = lax.broadcasted_iota(jnp.int32, (rows, dim), 1)
            row = lax.broadcasted_iota(jnp.int32, (rows, dim), 0)
            where = jnp.zeros((rows, dim), jnp.int32)
            for n in range(rows):
                where = jnp.where(row == n, position[n], where)
            angle = where.astype(F32) * freq[...]
            cosine = jnp.cos(angle)
            sine = jnp.sin(angle)
            sine = jnp.where(lane < dim // 2, -sine, sine)
            cos_out[...] = cosine
            sin_out[...] = sine
    for c in small[3:]:
        c.wait()
    request = lax.broadcasted_iota(jnp.int32, codes.shape, 1)
    code = (request * slots + slot_buf[...]) * SIZES + count_buf[...] // BLOCK
    codes[...] = jnp.where(owner_buf[...] == lax.axis_index("grp"), code, -1)
    cosine, sine = cos_out[...], sin_out[...]
    for n in range(acc.shape[1] // dim):
        v = rms_rope(acc[:, n * dim : (n + 1) * dim], q_gain[...], cosine, sine)
        heads_buf[:, n, :] = v * scale
    q_out[...] = heads_buf[...].astype(BF16)


def kv_kernel(normed, cosine, sine, k_gain, q, k_weight, v_weight, self_out, v_out, heads_buf):
    k_acc = jnp.dot(normed[...], k_weight[...], preferred_element_type=F32)
    v_acc = jnp.dot(normed[...], v_weight[...], preferred_element_type=F32)
    dim = k_gain.shape[-1]
    heads = q.shape[1]
    group = heads // (k_acc.shape[1] // dim)
    for n in range(heads):
        if n % group == 0:
            part = slice((n // group) * dim, (n // group + 1) * dim)
            k = rms_rope(k_acc[:, part], k_gain[...], cosine[...], sine[...])
            k = k.astype(BF16).astype(F32)
            v = v_acc[:, part].astype(BF16).astype(F32)
        heads_buf[:, n, :] = k
        v_out[:, n, :] = v
    score = jnp.sum(q[...].astype(F32) * heads_buf[...], axis=-1, keepdims=True)
    self_out[...] = jnp.broadcast_to(score, self_out.shape)


def text_parts(rows):
    return ((0, rows // 2), (rows // 2, rows))


def spread(q, kv_heads):
    group = q.shape[0] // kv_heads
    owner = lax.broadcasted_iota(jnp.int32, q.shape, 0) // group
    q = q.astype(F32)
    return jnp.concatenate(
        [jnp.where(owner == n, q, 0.0) for n in range(kv_heads)], axis=1
    ).astype(BF16)


def gather_heads(o, heads, dim):
    kv_heads = o.shape[1] // dim
    owner = lax.broadcasted_iota(jnp.int32, (heads, dim), 0) // (heads // kv_heads)
    total = jnp.zeros((heads, dim), F32)
    for n in range(kv_heads):
        total = jnp.where(owner == n, o[:, n * dim : (n + 1) * dim], total)
    return total


def score_block(q, keys, valid):
    scores = lax.dot_general(
        spread(q, keys.shape[1] // q.shape[1]), keys, (((1,), (1,)), ((), ())),
        preferred_element_type=F32,
    )
    return jnp.where(valid, scores, NEG)


def weigh_block(scores, values, heads, dim):
    top = jnp.max(scores, axis=-1, keepdims=True)
    weights = jnp.exp(scores - top).astype(BF16)
    total = jnp.sum(weights.astype(F32), axis=-1, keepdims=True)
    summed = jnp.dot(weights, values, preferred_element_type=F32)
    return top, total, gather_heads(summed, heads, dim)


def plan_kernel(slots, codes, item):
    def note(r, have):
        code = codes[0, r]
        hit = code >= 0
        item[jnp.where(hit, have, slots)] = code
        return have + hit.astype(jnp.int32)

    item[slots + 1] = lax.fori_loop(0, codes.shape[1], note, jnp.int32(0), unroll=16)


def text_kernel(
    first, q, position_in, keys, values, o_out, m_out, l_out, k_buf, v_buf, position, k_sem, v_sem,
    p_sem
):
    count, window, _ = k_buf.shape
    heads, dim = q.shape[1:]
    copies = [
        [
            pltpu.make_async_copy(src.at[first + i], dst.at[i], sem.at[i])
            for src, dst, sem in ((keys, k_buf, k_sem), (values, v_buf, v_sem))
        ]
        for i in range(count)
    ]
    table = pltpu.make_async_copy(position_in, position, p_sem)
    copies[0][0].start()
    table.start()
    copies[0][1].start()
    for pair in copies[1:]:
        for c in pair:
            c.start()
    table.wait()
    column = lax.broadcasted_iota(jnp.int32, (heads, window), 1)

    def score(i):
        p = position[first + i]
        valid = (column < p) & (column != lax.rem(p, window))
        return score_block(q[first + i], k_buf[i], valid)

    copies[0][0].wait()
    scores = score(0)
    for i in range(count):
        if i + 1 < count:
            copies[i + 1][0].wait()
        copies[i][1].wait()
        later = score(i + 1) if i + 1 < count else None
        top, total, summed = weigh_block(scores, v_buf[i], heads, dim)
        o_out[i] = summed
        m_out[i] = jnp.broadcast_to(top, summed.shape)
        l_out[i] = jnp.broadcast_to(total, summed.shape)
        scores = later


def image_kernel(batch, n_q, item, *refs):
    queries = refs[:n_q]
    keys, values, mine, other, q_buf, s_buf, out_buf = refs[n_q:]
    me = lax.axis_index("grp")
    slots, length, _ = keys.shape
    rows = queries[0].shape[0]
    heads, dim = queries[0].shape[1:]
    half = mine.shape[0]
    have = item[slots + 1]
    out_buf[...] = jnp.zeros_like(out_buf)
    known, step = [0], half
    q_buf[:rows] = queries[0][...]
    for ref in queries[1:]:
        new = [j ^ step for j in known]
        step //= 2
        for n, j in enumerate(new):
            q_buf[j * rows : (j + 1) * rows] = ref[n * rows : (n + 1) * rows]
        known = known + new
    column = lax.broadcasted_iota(jnp.int32, (heads, length), 1)
    lane_of = lax.broadcasted_iota(jnp.int32, (heads, dim), 1)

    def members(t):
        found = []
        for u in range(batch):
            n = t * batch + u
            live = n < have
            n = jnp.minimum(n, have - 1)
            code = item[n]
            both = code // SIZES
            r = both // slots
            found.append((live, r, both - r * slots, (code - both * SIZES) * BLOCK))
        return found

    def score(t):
        for u, (live, r, place, tokens) in enumerate(members(t)):
            group, lane = lax.bitwise_xor(r // rows, me), lax.rem(r, rows)
            s_buf[lax.rem(t, 2), u] = score_block(
                q_buf[group * rows + lane], keys[place], column < tokens
            )

    def weigh(t):
        done = []
        for u, (live, r, place, tokens) in enumerate(members(t)):
            top, total, summed = weigh_block(s_buf[lax.rem(t, 2), u], values[place], heads, dim)
            mean = (summed / total).astype(BF16)
            group, lane = lax.bitwise_xor(r // rows, me), lax.rem(r, rows)
            level = top + jnp.log(total)
            high = level.astype(BF16).astype(F32)
            middle = (level - high).astype(BF16).astype(F32)
            low = level - high - middle
            kind = lane_of - 3 * lane
            stats = jnp.where(
                kind == 0, high, jnp.where(kind == 1, middle, jnp.where(kind == 2, low, 0.0))
            )
            at = jnp.where(live, group, 2 * half) * (rows + 1)
            done.append((at + lane, at + rows, mean, stats))
        for at, stats_at, mean, stats in done:
            out_buf[at] = mean
            out_buf[stats_at] = (out_buf[stats_at].astype(F32) + stats).astype(BF16)

    last = (have + batch - 1) // batch - 1

    @pl.when(have > 0)
    def _():
        score(0)

        def both(t, carry):
            score(t + 1)
            weigh(t)
            return carry

        lax.fori_loop(0, last, both, 0)
        weigh(last)

    for j in range(half):
        for n in range(rows + 1):
            mine[j, n] = out_buf[2 * j * (rows + 1) + n]
            other[j, n] = out_buf[(2 * j + 1) * (rows + 1) + n]


def out_kernel(size, n_image, n_text, *refs):
    images = refs[:n_image]
    text = refs[n_image : n_image + n_text]
    own, v_new, weight, sent, kept, heads_buf, at_buf = refs[n_image + n_text :]
    rows, heads, dim = own.shape
    holds = [(n, i) for n in range(0, n_text, 3) for i in range(text[n].shape[0])]
    stats = images[0][rows].astype(F32)
    for ref in images[1:]:
        stats = stats + ref[rows].astype(F32)
    for r in range(rows):
        mean = images[0][r].astype(F32)
        for ref in images[1:]:
            mean = mean + ref[r].astype(F32)
        image_level = (
            stats[:, 3 * r : 3 * r + 1] + stats[:, 3 * r + 1 : 3 * r + 2]
        ) + stats[:, 3 * r + 2 : 3 * r + 3]
        part, at = holds[r]
        o_text, m, l_text = (ref[at] for ref in text[part : part + 3])
        s = own[r]
        top = jnp.maximum(jnp.maximum(image_level, m), s)
        e_image = jnp.exp(image_level - top)
        e_text = jnp.exp(m - top)
        e_own = jnp.exp(s - top)
        upper = mean * e_image + o_text * e_text + v_new[r] * e_own
        lower = e_image + l_text * e_text + e_own
        heads_buf[r] = upper / lower
    for n in range(heads):
        at_buf[:, n * dim : (n + 1) * dim] = heads_buf[:, n, :].astype(BF16)
    for i in range(weight.shape[0] // size):
        part = jnp.dot(
            at_buf[:, i * size : (i + 1) * size],
            weight[i * size : (i + 1) * size, :],
            preferred_element_type=F32,
        )
        if i == 0:
            kept[...] = part
        else:
            kept[...] += part
    sent[...] = kept[...].astype(BF16)


def final_kernel(n_others, *refs):
    others = refs[:n_others]
    kept, hidden, gain, out = refs[n_others:]
    y = kept[...]
    for ref in others:
        y = y + ref[...].astype(F32)
    mean_sq = jnp.sum(y * y, axis=-1, keepdims=True) / y.shape[1]
    scale = lax.rsqrt(mean_sq + EPS)
    width = out.shape[1]
    me = lax.axis_index("head")
    for n in range(y.shape[1] // width):
        @pl.when(me == n)
        def _():
            part = slice(n * width, (n + 1) * width)
            out[...] = (hidden[:, part].astype(F32) + y[:, part] * scale * gain[...]).astype(BF16)


def stay(x):
    return pltpu.with_memory_space_constraint(x, pltpu.HBM)


def swap(x, axis, k):
    n = lax.axis_size(axis)
    return lax.ppermute(x, axis, [(i, i ^ k) for i in range(n)])


def body(
    hidden, pre_gain, query_weight, key_weight, value_weight, out_weight, query_norm_gain, key_gain,
    post_gain, text_keys, text_values, text_position, image_keys, image_values, image_owner,
    image_slot, image_count,
):
    rows, width = hidden.shape
    dim = query_norm_gain.shape[0]
    heads = query_weight.shape[1] // dim
    groups = lax.axis_size("grp")
    head_parts = lax.axis_size("head")
    slots, length = image_keys.shape[0], image_keys.shape[1]
    scale = 1.0 / math.sqrt(width // (heads * head_parts))
    half = dim // 2
    freq = jnp.exp(-jnp.log(1000000.0) * jnp.arange(half, dtype=F32) / half)
    freq = jnp.concatenate([freq, freq])[None, :]

    size = pieces_of(width, 768)
    n_copies = width // size
    every = (1, groups * rows)
    q, normed, cosine, sine, k_gain, codes = pl.pallas_call(
        functools.partial(query_kernel, scale, size, slots),
        out_shape=(
            jax.ShapeDtypeStruct((rows, heads, dim), BF16),
            jax.ShapeDtypeStruct((rows, width), BF16),
            jax.ShapeDtypeStruct((rows, dim), F32),
            jax.ShapeDtypeStruct((rows, dim), F32),
            jax.ShapeDtypeStruct((1, dim), F32),
            jax.ShapeDtypeStruct(every, jnp.int32),
        ),
        in_specs=[VMEM] + [HBM] * 9,
        out_specs=(VMEM,) * 6,
        scratch_shapes=[
            pltpu.VMEM(query_weight.shape, BF16),
            pltpu.VMEM(hidden.shape, BF16),
            pltpu.VMEM((width // dim, dim), F32),
            pltpu.VMEM((1, dim), F32),
            pltpu.VMEM((rows, heads, dim), F32),
            pltpu.SMEM(text_position.shape, jnp.int32),
            pltpu.VMEM(every, jnp.int32),
            pltpu.VMEM(every, jnp.int32),
            pltpu.VMEM(every, jnp.int32),
            pltpu.SemaphoreType.DMA((n_copies,)),
            pltpu.SemaphoreType.DMA((8,)),
        ],
        compiler_params=pltpu.CompilerParams(vmem_limit_bytes=16 << 20),
        cost_estimate=cost(2 * rows * query_weight.size, 2 * query_weight.size),
        name="query",
    )(
        freq,
        *map(
            stay,
            (
                hidden, pre_gain.reshape(-1, dim), query_norm_gain.reshape(1, -1),
                key_gain.reshape(1, -1), text_position, image_owner.reshape(1, -1),
                image_count.reshape(1, -1), image_slot.reshape(1, -1), query_weight,
            ),
        ),
    )

    queries = [q]
    held = q
    k = groups // 2
    while k:
        got = swap(held, "grp", k)
        queries.append(got)
        k //= 2
        if k:
            held = jnp.concatenate([held, got], axis=0)

    text = []
    for first, last in text_parts(rows):
        part = (last - first,) + text_keys.shape[1:]
        share = math.prod(part)
        text += pl.pallas_call(
            functools.partial(text_kernel, first),
            out_shape=(jax.ShapeDtypeStruct((last - first, heads, dim), F32),) * 3,
            in_specs=[VMEM, HBM, HBM, HBM],
            out_specs=(VMEM,) * 3,
            scratch_shapes=[
                pltpu.VMEM(part, BF16),
                pltpu.VMEM(part, BF16),
                pltpu.SMEM(text_position.shape, jnp.int32),
                pltpu.SemaphoreType.DMA(part[:1]),
                pltpu.SemaphoreType.DMA(part[:1]),
                pltpu.SemaphoreType.DMA,
            ],
            compiler_params=pltpu.CompilerParams(vmem_limit_bytes=4 * share + SMALL),
            cost_estimate=cost(8 * heads * share, 4 * share),
        )(q, *map(stay, (text_position, text_keys, text_values)))

    item = pl.pallas_call(
        functools.partial(plan_kernel, slots),
        out_shape=jax.ShapeDtypeStruct((slots + 2,), jnp.int32),
        in_specs=[SMEM],
        out_specs=SMEM,
        compiler_params=pltpu.CompilerParams(vmem_limit_bytes=SMALL),
        cost_estimate=cost(1 << 20, 1 << 20),
        name="plan",
    )(codes)

    batch = 8
    mine, other = pl.pallas_call(
        functools.partial(image_kernel, batch, len(queries)),
        out_shape=(jax.ShapeDtypeStruct((groups // 2, rows + 1, heads, dim), BF16),) * 2,
        in_specs=[SMEM] + [VMEM] * (len(queries) + 2),
        out_specs=(VMEM, VMEM),
        scratch_shapes=[
            pltpu.VMEM((groups * rows, heads, dim), BF16),
            pltpu.VMEM((2, batch, heads, length), F32),
            pltpu.VMEM(((groups + 1) * (rows + 1), heads, dim), BF16),
        ],
        compiler_params=pltpu.CompilerParams(vmem_limit_bytes=SMALL),
        cost_estimate=cost(8 * heads * image_keys.size, 4 * image_keys.size),
        name="image",
    )(item, *queries, image_keys, image_values)

    key_weight, value_weight, out_weight, mine, other = lax.optimization_barrier(
        (key_weight, value_weight, out_weight, mine, other)
    )
    own_score, v_new = pl.pallas_call(
        kv_kernel,
        out_shape=(jax.ShapeDtypeStruct((rows, heads, dim), F32),) * 2,
        in_specs=[VMEM] * 7,
        out_specs=(VMEM, VMEM),
        scratch_shapes=[pltpu.VMEM((rows, heads, dim), F32)],
        compiler_params=pltpu.CompilerParams(vmem_limit_bytes=SMALL),
        cost_estimate=cost(4 * rows * key_weight.size, 4 * key_weight.size),
        name="keyvalue",
    )(normed, cosine, sine, k_gain, q, key_weight, value_weight)

    got = swap(other, "grp", 1)
    images = []
    for j in range(groups // 2):
        moved = mine[j] + got[j]
        images.append(swap(moved, "grp", 2 * j) if j else moved)

    o_size = pieces_of(out_weight.shape[0], 256)
    sent, kept = pl.pallas_call(
        functools.partial(out_kernel, o_size, len(images), len(text)),
        out_shape=(
            jax.ShapeDtypeStruct((rows, width), BF16),
            jax.ShapeDtypeStruct((rows, width), F32),
        ),
        in_specs=[VMEM] * (len(images) + len(text) + 3),
        out_specs=(VMEM, VMEM),
        scratch_shapes=[pltpu.VMEM((rows, heads, dim), F32), pltpu.VMEM((rows, heads * dim), BF16)],
        compiler_params=pltpu.CompilerParams(vmem_limit_bytes=SMALL),
        cost_estimate=cost(2 * rows * out_weight.size, 2 * out_weight.size),
        name="project",
    )(*images, *text, own_score, v_new, out_weight)

    others = [swap(sent, "head", j) for j in range(1, head_parts)]
    return pl.pallas_call(
        functools.partial(final_kernel, len(others)),
        out_shape=jax.ShapeDtypeStruct((rows, width // head_parts), BF16),
        in_specs=[VMEM] * (len(others) + 3),
        out_specs=VMEM,
        compiler_params=pltpu.CompilerParams(vmem_limit_bytes=SMALL),
        cost_estimate=cost(8 * rows * width, 16 * rows * width),
        name="finish",
    )(*others, kept, hidden, post_gain.reshape(1, -1))


def solution(mesh):
    placed = (
        P("grp", None),
        P(),
        P(None, "head"),
        P(None, "head"),
        P(None, "head"),
        P("head", None),
        P(),
        P(),
        P("head"),
        P("grp", None, "head"),
        P("grp", None, "head"),
        P("grp"),
        P("grp", None, "head"),
        P("grp", None, "head"),
        P(),
        P(),
        P(),
    )
    return jax.shard_map(
        body, mesh=mesh, in_specs=placed, out_specs=P("grp", "head"), check_vma=False
    )
```
